256 devices in a mesh: expert: 128 (over y, x, z), dp: 2 (over core).
Axes of the slice: x: 4, y: 4, z: 8, core: 2. Of those that a mesh axis runs over, the one named last changes fastest.
Arguments:
- tokens: bfloat16 [4096, 2048], P(('dp', 'expert')), parts along dimension 0, may hold values from -6 to 6
- expert_ids: int32 [4096, 8], P(('dp', 'expert')), parts along dimension 0, may hold values from 0 to 127, all different within a row; in each aligned block of 16 rows (0 to 15, 16 to 31, ...) at most 2 rows name the same one
- gate_values: float32 [4096, 8], P(('dp', 'expert')), parts along dimension 0, may hold values from 0.03 to 0.4
- w_gate: bfloat16 [128, 2048, 768], P('expert'), may hold values from -0.125 to 0.125
- w_up: bfloat16 [128, 2048, 768], P('expert'), may hold values from -0.125 to 0.125
- w_down: bfloat16 [128, 768, 2048], P('expert'), may hold values from -0.21875 to 0.21875
- cotangent: bfloat16 [4096, 2048], P(('dp', 'expert')), parts along dimension 0, may hold values from -6 to 6
Outputs:
- mixed_rows: bfloat16 [4096, 2048], P(('dp', 'expert')), parts along dimension 0
- row_grads: bfloat16 [4096, 2048], P(('dp', 'expert')), parts along dimension 0
- gate_grads: float32 [4096, 8], P(('dp', 'expert')), parts along dimension 0
The draws below stay inside these ranges and needn't reach their ends.
There are 2 independent parts, one for each index of `dp`. The reference program is written for one: setup_inputs(seed, part) draws one part's arguments, and reference() takes and returns one part's arrays. A program takes and returns all parts, laid end to end along the dimension named above; an argument that names none is the same for every part. Nothing has to cross between parts.
Inputs may be any that keep to these rules, and one draw needn't show every extreme that they name: `expert_ids`: each token names 8 different experts. Among the 16 tokens of one device no expert is named more than 2 times, and in every draw some device names some expert exactly 2 times.
All inputs are finite; a program needn't handle non-finite values.
Results may differ from the reference program's by a relative error of at most 0.0064.
Values may be sent and summed in bfloat16 or wider, within the bound.
No kernel may reach another device: no remote copies, remote signals or barrier semaphores. Data moves between devices by JAX's collectives and lax.ppermute only.
A program may use at most 128 MiB of HBM per device.

```python
import math
import jax
import jax.numpy as jnp
import numpy as np
from jax import lax

D = 2048
FF = 768
TOP = 8
TOK_DEV = 16
EXPERTS = 128
TOKENS = 2048
MOST = 2


def shard_levels(own_key, extent, pieces, least, top_value):
    def one(dim, parts):
        steps = jax.random.uniform(jax.random.fold_in(jax.random.fold_in(own_key, 6), dim), (parts,), jnp.float32, least / len(pieces), top_value / len(pieces))
        return jnp.repeat(jnp.exp(steps), extent[dim] // parts).reshape((-1,) + (1,) * (len(extent) - dim - 1))

    gain = one(*pieces[0])
    for cut in pieces[1:]:
        gain = gain * one(*cut)
    return gain


def shared_out(own_key, own, number, rows, number_of, top, bound, lean):
    ranking = jax.random.permutation(own_key, number_of)
    heavy_load, ordinary = shares(number_of, rows * top, bound, lean, True), shares(number_of, rows * top, bound, lean, False)
    places = jnp.arange(number_of)

    def named(sizes, rotation):
        used = int((sizes > 0).sum())
        fixed = max(1, used // 4)
        shifted = fixed + (places - fixed + rotation * (used - fixed)) % max(1, number_of - fixed)
        return jnp.zeros((number_of,), jnp.int32).at[ranking[jnp.where(places < fixed, places, shifted)]].set(jnp.asarray(sizes, jnp.int32))

    sizes = jnp.where(number % 4 == 0, named(heavy_load, number // 4), named(ordinary, number - number // 4 - 1))
    mixed = jax.random.permutation(jax.random.fold_in(own, 3), number_of)
    donor, sink = mixed[0:number_of // 2 * 2:2], mixed[1:number_of // 2 * 2:2]
    slack = jnp.minimum(sizes[donor] - 1, bound - sizes[sink]) // 2
    slack = jnp.where((donor == ranking[0]) | (sink == ranking[0]) | (sizes[sink] == 0), 0, jnp.maximum(slack, 0))
    shifted = jax.random.randint(jax.random.fold_in(own, 4), (number_of // 2,), 0, 1 << 20) % (slack + 1)
    sizes = sizes.at[donor].add(-shifted).at[sink].add(shifted)
    labels = jnp.searchsorted(jnp.cumsum(sizes), jnp.arange(rows * top), side="right").astype(jnp.int32)
    table = labels.reshape(top, rows).T
    table = table[jax.random.permutation(jax.random.fold_in(own, 1), rows)]
    rotation = jax.random.randint(jax.random.fold_in(own, 2), (rows, 1), 0, top)
    return jnp.take_along_axis(table, (jnp.arange(top)[None, :] + rotation) % top, axis=1)


def shares(number_of, total, most, skew, full):
    weights = [(1 << 20) // math.isqrt(standing ** skew) + 1 for standing in range(1, number_of + 1)]
    largest = most if full else min(most, max(-(-total // number_of), total * weights[0] // sum(weights)))
    least = 1 if total - largest >= number_of - 1 else 0
    given, rest = [largest] + [least] * (number_of - 1), total - largest - least * (number_of - 1)
    while rest > 0:
        free = [i for i in range(1, number_of) if given[i] < largest] or [i for i in range(1, number_of) if given[i] < most]
        pool, remaining = sum([weights[i] for i in free]), rest
        for i in free:
            more = min(most - given[i], max(1, remaining * weights[i] // pool), rest)
            given[i] = given[i] + more
            rest = rest - more
    return np.array(given)


def scatter_about(key, extent, spread, reach, pieces=(), held_as=jnp.bfloat16):
    array = jax.random.normal(key, extent, jnp.float32) * spread
    if len(pieces) > 0:
        array = shard_levels(key, extent, pieces, -0.22, 0.18) * array
    return jnp.clip(array, min=-reach, max=reach).astype(held_as)


def setup_inputs(seed: int = 0, part: int = 0) -> dict:
    seeds = jax.random.split(jax.random.key(seed), 8)
    part_splits = jax.random.split(jax.random.fold_in(seeds[7], part), 8)
    tokens = scatter_about(part_splits[0], (TOKENS, D), 1.0, 6.0, ((0, 128),))
    expert_ids_keys = jax.random.split(jax.random.fold_in(part_splits[1], 1), TOKENS // TOK_DEV)
    expert_ids_turns = jax.random.permutation(jax.random.fold_in(part_splits[1], 3), TOKENS // TOK_DEV)
    expert_ids = jax.vmap(lambda own, number: shared_out(jax.random.fold_in(part_splits[1], 2), own, number, TOK_DEV, EXPERTS, TOP, MOST, 2))(expert_ids_keys, expert_ids_turns).reshape((TOKENS, TOP))
    gate_values = jnp.clip(jnp.exp(math.log(0.4) - 2.5902672 * jax.random.uniform(part_splits[2], (TOKENS, TOP), jnp.float32) ** shard_levels(part_splits[2], (TOKENS, TOP), ((0, 128),), -0.2, 0.2)), 0.03, 0.4)
    w_gate = scatter_about(seeds[3], (EXPERTS, D, FF), D ** -0.5, 0.125, ((0, 128),))
    w_up = scatter_about(seeds[4], (EXPERTS, D, FF), D ** -0.5, 0.125, ((0, 128),))
    w_down = scatter_about(seeds[5], (EXPERTS, FF, D), FF ** -0.5, 0.21875, ((0, 128),))
    cotangent = scatter_about(part_splits[6], (TOKENS, D), 1.0, 6.0, ((0, 128),))
    return {"tokens": tokens, "expert_ids": expert_ids, "gate_values": gate_values, "w_gate": w_gate, "w_up": w_up, "w_down": w_down, "cotangent": cotangent}


def expert_forward(inputs, gate_matrix, up_matrix, down_matrix):
    pre_gate = jnp.dot(inputs, gate_matrix, preferred_element_type=jnp.float32)
    pre_up = jnp.dot(inputs, up_matrix, preferred_element_type=jnp.float32)
    hidden = (pre_gate * jax.nn.sigmoid(pre_gate) * pre_up).astype(jnp.bfloat16)
    output = jnp.dot(hidden, down_matrix, preferred_element_type=jnp.float32).astype(jnp.bfloat16)
    return output, pre_gate, pre_up


def expert_backward(grad_output, pre_gate, pre_up, gate_matrix, up_matrix, down_matrix):
    contract = (((1,), (1,)), ((), ()))
    grad_hidden = lax.dot_general(grad_output, down_matrix, contract, preferred_element_type=jnp.float32)
    sigmoid = jax.nn.sigmoid(pre_gate)
    grad_gate = (grad_hidden * pre_up * sigmoid * (1.0 + pre_gate * (1.0 - sigmoid))).astype(jnp.bfloat16)
    grad_up = (grad_hidden * pre_gate * sigmoid).astype(jnp.bfloat16)
    first_part = lax.dot_general(grad_gate, gate_matrix, contract, preferred_element_type=jnp.float32)
    second_part = lax.dot_general(grad_up, up_matrix, contract, preferred_element_type=jnp.float32)
    return (first_part + second_part).astype(jnp.bfloat16)


def reference(tokens, expert_ids, gate_values, w_gate, w_up, w_down, cotangent):
    flat_ids = expert_ids.reshape(-1).astype(jnp.int32)
    entry_total = flat_ids.shape[0]
    capacity = EXPERTS * MOST
    model_width = tokens.shape[1]
    padding = jnp.zeros((1, model_width), jnp.bfloat16)
    tokens_pad = jnp.concatenate([tokens, padding], axis=0)
    cotangent_pad = jnp.concatenate([cotangent, padding], axis=0)
    gates_pad = jnp.concatenate([gate_values.reshape(-1), jnp.zeros((1,), jnp.float32)])
    positions = jnp.arange(entry_total, dtype=jnp.int32)

    def per_expert(running, which_expert):
        mixed_sum, grad_sum, gate_grads = running
        matches = (flat_ids == which_expert).astype(jnp.int32)
        ranked = jnp.cumsum(matches) - matches
        placed = jnp.where(matches == 1, ranked, capacity).astype(jnp.int32)
        slot_table = jnp.full((capacity + 1,), entry_total, jnp.int32).at[placed].set(positions)[:capacity]
        token_index = (slot_table // TOP).astype(jnp.int32)
        inputs = tokens_pad[token_index]
        output, pre_gate, pre_up = expert_forward(inputs, w_gate[which_expert], w_up[which_expert], w_down[which_expert])
        weights = gates_pad[slot_table]
        output_wide = output.astype(jnp.float32)
        mixed_sum = mixed_sum.at[token_index].add(weights[:, None] * output_wide, mode="drop")
        upstream = cotangent_pad[token_index].astype(jnp.float32)
        gate_grads = gate_grads.at[slot_table].set(jnp.sum(upstream * output_wide, axis=1), mode="drop")
        grad_output = (weights[:, None] * upstream).astype(jnp.bfloat16)
        grad_rows = expert_backward(grad_output, pre_gate, pre_up, w_gate[which_expert], w_up[which_expert], w_down[which_expert])
        grad_sum = grad_sum.at[token_index].add(grad_rows.astype(jnp.float32), mode="drop")
        return (mixed_sum, grad_sum, gate_grads), None

    start_state = (jnp.zeros(tokens.shape, jnp.float32), jnp.zeros(tokens.shape, jnp.float32), jnp.zeros((entry_total,), jnp.float32))
    final_state, _ = lax.scan(per_expert, start_state, jnp.arange(EXPERTS, dtype=jnp.int32))
    mixed_sum, grad_sum, gate_grads = final_state
    return mixed_sum.astype(jnp.bfloat16), grad_sum.astype(jnp.bfloat16), gate_grads.reshape(expert_ids.shape)
```

```python
import jax
import jax.numpy as jnp
from jax import lax
from jax.sharding import PartitionSpec as P


def expert_forward(inputs, gate_matrix, up_matrix, down_matrix):
    pre_gate = jnp.dot(inputs, gate_matrix, preferred_element_type=jnp.float32)
    pre_up = jnp.dot(inputs, up_matrix, preferred_element_type=jnp.float32)
    hidden = (pre_gate * jax.nn.sigmoid(pre_gate) * pre_up).astype(jnp.bfloat16)
    output = jnp.dot(hidden, down_matrix, preferred_element_type=jnp.float32).astype(jnp.bfloat16)
    return (output, pre_gate, pre_up)


def expert_backward(grad_output, pre_gate, pre_up, gate_matrix, up_matrix, down_matrix):
    contract = (((1,), (1,)), ((), ()))
    grad_hidden = lax.dot_general(
        grad_output, down_matrix, contract, preferred_element_type=jnp.float32
    )
    sigmoid = jax.nn.sigmoid(pre_gate)
    grad_gate = (grad_hidden * pre_up * sigmoid * (1.0 + pre_gate * (1.0 - sigmoid))).astype(
        jnp.bfloat16
    )
    grad_up = (grad_hidden * pre_gate * sigmoid).astype(jnp.bfloat16)
    first_part = lax.dot_general(
        grad_gate, gate_matrix, contract, preferred_element_type=jnp.float32
    )
    second_part = lax.dot_general(grad_up, up_matrix, contract, preferred_element_type=jnp.float32)
    return (first_part + second_part).astype(jnp.bfloat16)


def split_three(values):
    high = lax.reduce_precision(values, 8, 7)
    rest = values - high
    middle = lax.reduce_precision(rest, 8, 7)
    low = lax.reduce_precision(rest - middle, 8, 7)
    return high, middle, low


def exchange(rows, experts, capacity):
    width = rows.shape[1]
    return lax.all_to_all(
        rows.reshape(experts, capacity, width), "expert", split_axis=0, concat_axis=0, tiled=True
    ).reshape(experts * capacity, width)


def local(tokens, expert_ids, gate_values, w_gate, w_up, w_down, cotangent):
    row_count, _ = tokens.shape
    top_count = expert_ids.shape[1]
    experts = lax.axis_size("expert")
    capacity = 2
    slot_total = experts * capacity
    entry_count = row_count * top_count
    gate_matrix = w_gate[0]
    up_matrix = w_up[0]
    down_matrix = w_down[0]
    ids = expert_ids.T.reshape(-1)
    gates = gate_values.T.reshape(-1)
    order = jnp.arange(entry_count, dtype=jnp.int32)
    earlier = (ids[:, None] == ids[None, :]) & (order[:, None] < order[None, :])
    ranked = jnp.sum(earlier.astype(jnp.int32), axis=0)
    places = ids * capacity + ranked
    slots = jnp.arange(slot_total, dtype=jnp.int32)
    hit = slots[:, None] == places[None, :]
    hit_by = hit.reshape(slot_total, top_count, row_count)
    select = jnp.any(hit_by, axis=1).astype(jnp.bfloat16)
    slot_gates = jnp.sum(jnp.where(hit, gates[None, :], 0.0), axis=1)
    weights = jnp.sum(
        jnp.where(hit_by, gates.reshape(1, top_count, row_count), 0.0), axis=1
    )
    sent_rows = jnp.dot(select, tokens, preferred_element_type=jnp.float32).astype(jnp.bfloat16)
    sent_grads = (
        slot_gates[:, None] * jnp.dot(select, cotangent, preferred_element_type=jnp.float32)
    ).astype(jnp.bfloat16)
    received = exchange(sent_rows, experts, capacity)
    incoming = exchange(sent_grads, experts, capacity)
    output, pre_gate, pre_up = expert_forward(received, gate_matrix, up_matrix, down_matrix)
    returned = exchange(output, experts, capacity)
    grad_rows = expert_backward(incoming, pre_gate, pre_up, gate_matrix, up_matrix, down_matrix)
    returned_grads = exchange(grad_rows, experts, capacity)
    over_slots = (((0,), (0,)), ((), ()))
    parts = jnp.concatenate([part.astype(jnp.bfloat16) for part in split_three(weights)], axis=1)
    mixed = lax.dot_general(parts, returned, over_slots, preferred_element_type=jnp.float32)
    mixed = mixed.reshape(3, row_count, -1)
    mixed_rows = (mixed[2] + mixed[1] + mixed[0]).astype(jnp.bfloat16)
    scores = lax.dot_general(
        cotangent, returned, (((1,), (1,)), ((), ())), preferred_element_type=jnp.float32
    )
    picked = jnp.where(hit_by, scores.T[:, None, :], 0.0)
    gate_grads = jnp.sum(picked, axis=0).T
    row_grads = lax.dot_general(
        select, returned_grads, over_slots, preferred_element_type=jnp.float32
    ).astype(jnp.bfloat16)
    return (mixed_rows, row_grads, gate_grads)


def solution(mesh):
    return jax.shard_map(
        local,
        mesh=mesh,
        in_specs=(
            P(("dp", "expert"), None),
            P(("dp", "expert"), None),
            P(("dp", "expert"), None),
            P("expert", None, None),
            P("expert", None, None),
            P("expert", None, None),
            P(("dp", "expert"), None),
        ),
        out_specs=(P(("dp", "expert"), None), P(("dp", "expert"), None), P(("dp", "expert"), None)),
        check_vma=False,
    )
```

```python
import jax
import jax.numpy as jnp
from jax import lax
from jax.experimental import pallas as pl
from jax.experimental.pallas import tpu as pltpu
from jax.sharding import PartitionSpec as P

DEPTH = 8
PLANE = 16
CAPACITY = 2
PLANE_STEP = 15
DEPTH_STEP = 3
ROWS = 16
TOP = 8
WIDTH = 2048
HIDDEN = 768
NOTES = 128
LINE = DEPTH * ROWS
EACH = DEPTH * CAPACITY
SLOTS = PLANE * EACH
BF = jnp.bfloat16
F32 = jnp.float32
COLUMNS = 512
MIB = 1024 * 1024


def iota(shape, dim):
    return lax.broadcasted_iota(jnp.int32, shape, dim)


def parts_of(values):
    high = values.astype(BF)
    rest = values - high.astype(F32)
    middle = rest.astype(BF)
    low = (rest - middle.astype(F32)).astype(BF)
    return high, middle, low


def pack_kernel(tokens_ref, cotangent_ref, ids_ref, gates_ref, out_ref):
    high, middle, low = parts_of(gates_ref[...])
    columns = jnp.concatenate(
        [ids_ref[...].astype(F32), high.astype(F32), middle.astype(F32), low.astype(F32)], axis=0
    )
    columns = jnp.concatenate([columns, jnp.zeros((NOTES - 4 * TOP, ROWS), F32)], axis=0)
    notes = columns.T.astype(BF)
    for start in range(0, LINE, ROWS):
        out_ref[start : start + ROWS, :WIDTH] = tokens_ref[...]
        out_ref[start : start + ROWS, WIDTH : 2 * WIDTH] = cotangent_ref[...]
        out_ref[start : start + ROWS, 2 * WIDTH :] = notes


def tables(depth, notes):
    notes = notes.astype(F32)
    lane = iota((LINE, SLOTS), 1)
    row = iota((LINE, SLOTS), 0)
    named = ((lane // EACH * PLANE_STEP % PLANE) * DEPTH + depth).astype(F32)
    matches = []
    weight = jnp.zeros((LINE, SLOTS), F32)
    member = jnp.zeros((LINE, SLOTS), F32)
    for k in range(TOP):
        match = notes[:, k : k + 1] == named
        gate = (
            notes[:, TOP + k : TOP + k + 1]
            + notes[:, 2 * TOP + k : 2 * TOP + k + 1]
            + notes[:, 3 * TOP + k : 3 * TOP + k + 1]
        )
        weight = jnp.where(match, gate, weight)
        member = jnp.where(match, 1.0, member)
        matches.append(match)
    left = iota((LINE, LINE), 0)
    right = iota((LINE, LINE), 1)
    ahead = ((left // ROWS == right // ROWS) & (right < left)).astype(F32).astype(BF)
    ranked = jnp.dot(ahead, member.astype(BF), preferred_element_type=F32)
    here = (row // ROWS == (lane % EACH) // CAPACITY) & (
        ranked == (lane % CAPACITY).astype(F32)
    )
    hit = jnp.where(here, member, 0.0)
    return hit, hit * weight, matches


def dispatch_kernel(depth_ref, line_ref, out_ref):
    notes = line_ref[:, 2 * WIDTH :]
    hit, weight, _ = tables(depth_ref[0], notes)
    select = hit.T.astype(BF)
    gates = jnp.sum(weight.T, axis=1, keepdims=True)
    for start in range(0, WIDTH, COLUMNS):
        block = line_ref[:, start : start + COLUMNS]
        out_ref[:, start : start + COLUMNS] = jnp.dot(
            select, block, preferred_element_type=F32
        ).astype(BF)
    for start in range(WIDTH, 2 * WIDTH, COLUMNS):
        block = line_ref[:, start : start + COLUMNS]
        out_ref[:, start : start + COLUMNS] = (
            gates * jnp.dot(select, block, preferred_element_type=F32)
        ).astype(BF)


def dot_t(left, right):
    return lax.dot_general(left, right, (((1,), (1,)), ((), ())), preferred_element_type=F32)


def expert_kernel(rows, gate_hbm, up_hbm, down_hbm, out, gate, up, down, sems):
    copies = [
        pltpu.make_async_copy(gate_hbm, gate, sems.at[0]),
        pltpu.make_async_copy(up_hbm, up, sems.at[1]),
        pltpu.make_async_copy(down_hbm, down, sems.at[2]),
    ]
    for copy in copies:
        copy.start()
    inputs = rows[:, :WIDTH]
    copies[0].wait()
    pre_gate = jnp.dot(inputs, gate[...], preferred_element_type=F32)
    copies[1].wait()
    pre_up = jnp.dot(inputs, up[...], preferred_element_type=F32)
    sigmoid = jax.nn.sigmoid(pre_gate)
    hidden = (pre_gate * sigmoid * pre_up).astype(BF)
    copies[2].wait()
    out[:, :WIDTH] = jnp.dot(hidden, down[...], preferred_element_type=F32).astype(BF)
    grad_hidden = dot_t(rows[:, WIDTH:], down[...])
    grad_gate = (grad_hidden * pre_up * sigmoid * (1.0 + pre_gate * (1.0 - sigmoid))).astype(BF)
    grad_up = (grad_hidden * pre_gate * sigmoid).astype(BF)
    out[:, WIDTH:] = (dot_t(grad_gate, gate[...]) + dot_t(grad_up, up[...])).astype(BF)


def combine_kernel(depth_ref, line_ref, back_ref, out_ref):
    hit, weight, matches = tables(depth_ref[0], line_ref[:, 2 * WIDTH :])
    select = hit.astype(BF)
    high, middle, low = parts_of(weight)
    scores = jnp.zeros((LINE, SLOTS), F32)
    for start in range(0, WIDTH, COLUMNS):
        block = back_ref[:, start : start + COLUMNS]
        mixed = (
            jnp.dot(low, block, preferred_element_type=F32)
            + jnp.dot(middle, block, preferred_element_type=F32)
            + jnp.dot(high, block, preferred_element_type=F32)
        )
        out_ref[:, start : start + COLUMNS] = mixed.astype(BF)
        scores = scores + dot_t(line_ref[:, WIDTH + start : WIDTH + start + COLUMNS], block)
    for start in range(WIDTH, 2 * WIDTH, COLUMNS):
        block = back_ref[:, start : start + COLUMNS]
        out_ref[:, start : start + COLUMNS] = jnp.dot(
            select, block, preferred_element_type=F32
        ).astype(BF)
    scores = jnp.where(hit > 0.0, scores, 0.0)
    lane = iota((LINE, NOTES), 1)
    notes = jnp.zeros((LINE, NOTES), F32)
    for k in range(TOP):
        total = jnp.sum(jnp.where(matches[k], scores, 0.0), axis=1, keepdims=True)
        for part, value in enumerate(parts_of(total)):
            notes = jnp.where(lane == part * TOP + k, value.astype(F32), notes)
    out_ref[:, 2 * WIDTH :] = notes.astype(BF)


def finish_kernel(parts_ref, mixed_ref, rows_ref, gates_ref):
    def total(start, stop):
        value = parts_ref[0, :, start:stop].astype(F32)
        for place in range(1, DEPTH):
            value = value + parts_ref[place, :, start:stop].astype(F32)
        return value

    mixed_ref[...] = total(0, WIDTH).astype(BF)
    rows_ref[...] = total(WIDTH, 2 * WIDTH).astype(BF)
    columns = total(2 * WIDTH, 2 * WIDTH + NOTES).T
    gates_ref[...] = columns[:TOP] + columns[TOP : 2 * TOP] + columns[2 * TOP : 3 * TOP]


def local(tokens, expert_ids, gate_values, w_gate, w_up, w_down, cotangent):
    total = 2 * WIDTH + NOTES
    place = lax.axis_index("expert")
    depth = (place % DEPTH).astype(jnp.int32).reshape(1)
    spots = [PLANE_STEP * spot % PLANE for spot in range(PLANE)]
    levels = [DEPTH_STEP * level % DEPTH for level in range(DEPTH)]
    planes = [[spot * DEPTH + level for spot in spots] for level in range(DEPTH)]
    lines = [[spot * DEPTH + level for level in levels] for spot in range(PLANE)]

    def exchange(blocks, groups):
        return lax.all_to_all(
            blocks, "expert", split_axis=0, concat_axis=0, tiled=True, axis_index_groups=groups
        )

    def near(array):
        return pltpu.with_memory_space_constraint(array, pltpu.VMEM)

    vmem = pl.BlockSpec(memory_space=pltpu.VMEM)
    smem = pl.BlockSpec(memory_space=pltpu.SMEM)
    anywhere = pl.BlockSpec(memory_space=pl.ANY)
    packed = pl.pallas_call(
        pack_kernel,
        out_shape=pltpu.VMEM((LINE, total), BF),
        in_specs=[vmem] * 4,
        out_specs=vmem,
        name="pack",
        compiler_params=pltpu.CompilerParams(vmem_limit_bytes=8 * MIB),
    )(tokens, cotangent, expert_ids.T, gate_values.T)
    line = near(exchange(packed.reshape(DEPTH, ROWS, total), lines).reshape(LINE, total))
    sent = pl.pallas_call(
        dispatch_kernel,
        out_shape=pltpu.VMEM((SLOTS, 2 * WIDTH), BF),
        in_specs=[smem, vmem],
        out_specs=vmem,
        name="dispatch",
        compiler_params=pltpu.CompilerParams(vmem_limit_bytes=16 * MIB),
    )(depth, line)
    received = exchange(sent.reshape(PLANE, EACH, 2 * WIDTH), planes)
    received = near(received.reshape(SLOTS, 2 * WIDTH))
    output = pl.pallas_call(
        expert_kernel,
        out_shape=pltpu.VMEM((SLOTS, 2 * WIDTH), BF),
        in_specs=[vmem, anywhere, anywhere, anywhere],
        out_specs=vmem,
        scratch_shapes=[
            pltpu.VMEM((WIDTH, HIDDEN), BF),
            pltpu.VMEM((WIDTH, HIDDEN), BF),
            pltpu.VMEM((HIDDEN, WIDTH), BF),
            pltpu.SemaphoreType.DMA((3,)),
        ],
        name="expert",
        compiler_params=pltpu.CompilerParams(vmem_limit_bytes=28 * MIB),
    )(received, w_gate[0], w_up[0], w_down[0])
    back = exchange(output.reshape(PLANE, EACH, 2 * WIDTH), planes)
    back = near(back.reshape(SLOTS, 2 * WIDTH))
    parts = pl.pallas_call(
        combine_kernel,
        out_shape=pltpu.VMEM((LINE, total), BF),
        in_specs=[smem, vmem, vmem],
        out_specs=vmem,
        name="combine",
        compiler_params=pltpu.CompilerParams(vmem_limit_bytes=16 * MIB),
    )(depth, line, back)
    parts = near(exchange(parts.reshape(DEPTH, ROWS, total), lines))
    mixed_rows, row_grads, gate_grads = pl.pallas_call(
        finish_kernel,
        out_shape=(
            jax.ShapeDtypeStruct((ROWS, WIDTH), BF),
            jax.ShapeDtypeStruct((ROWS, WIDTH), BF),
            jax.ShapeDtypeStruct((TOP, ROWS), F32),
        ),
        in_specs=[vmem],
        out_specs=(vmem, vmem, vmem),
        name="finish",
        compiler_params=pltpu.CompilerParams(vmem_limit_bytes=8 * MIB),
    )(parts)
    return (mixed_rows, row_grads, gate_grads.T)


def solution(mesh):
    return jax.shard_map(
        local,
        mesh=mesh,
        in_specs=(
            P(("dp", "expert"), None),
            P(("dp", "expert"), None),
            P(("dp", "expert"), None),
            P("expert", None, None),
            P("expert", None, None),
            P("expert", None, None),
            P(("dp", "expert"), None),
        ),
        out_specs=(P(("dp", "expert"), None), P(("dp", "expert"), None), P(("dp", "expert"), None)),
        check_vma=False,
    )
```

```python
import jax
import jax.numpy as jnp
from jax import lax
from jax.experimental import pallas as pl
from jax.experimental.pallas import tpu as pltpu
from jax.sharding import PartitionSpec as P

DEPTH = 8
PLANE = 16
EXPERTS = 128
CAPACITY = 2
PLANE_STEP = 15
DEPTH_STEP = 3
ROWS = 16
TOP = 8
WIDTH = 2048
HIDDEN = 768
NOTES = 128
LINE = DEPTH * ROWS
EACH = DEPTH * CAPACITY
SLOTS = PLANE * EACH
BF = jnp.bfloat16
F32 = jnp.float32
COLUMNS = 512
MIB = 1024 * 1024


def iota(shape, dim):
    return lax.broadcasted_iota(jnp.int32, shape, dim)


def parts_of(values):
    high = values.astype(BF)
    rest = values - high.astype(F32)
    middle = rest.astype(BF)
    low = (rest - middle.astype(F32)).astype(BF)
    return high, middle, low


def pack_kernel(tokens_ref, cotangent_ref, ids_ref, gates_ref, out_ref):
    high, middle, low = parts_of(gates_ref[...])
    columns = jnp.concatenate(
        [ids_ref[...].astype(F32), high.astype(F32), middle.astype(F32), low.astype(F32)], axis=0
    )
    columns = jnp.concatenate([columns, jnp.zeros((NOTES - 4 * TOP, ROWS), F32)], axis=0)
    notes = columns.T.astype(BF)
    for start in range(0, LINE, ROWS):
        out_ref[start : start + ROWS, :WIDTH] = tokens_ref[...]
        out_ref[start : start + ROWS, WIDTH : 2 * WIDTH] = cotangent_ref[...]
        out_ref[start : start + ROWS, 2 * WIDTH :] = notes


def tables(depth, notes):
    notes = notes.astype(F32)
    lane = iota((LINE, SLOTS), 1)
    row = iota((LINE, SLOTS), 0)
    member_of = lane // EACH
    core, place = depth // EXPERTS, depth % EXPERTS
    here = (member_of * PLANE_STEP % PLANE) * DEPTH + place % DEPTH
    other = (place // (4 * DEPTH)) * (4 * DEPTH) + (place // DEPTH % 2) * DEPTH
    other = other + (member_of % 2) * (2 * DEPTH) + member_of // 2
    named = jnp.where(core == 0, here, other).astype(F32)
    matches = []
    weight = jnp.zeros((LINE, SLOTS), F32)
    member = jnp.zeros((LINE, SLOTS), F32)
    for k in range(TOP):
        match = notes[:, k : k + 1] == named
        gate = (
            notes[:, TOP + k : TOP + k + 1]
            + notes[:, 2 * TOP + k : 2 * TOP + k + 1]
            + notes[:, 3 * TOP + k : 3 * TOP + k + 1]
        )
        weight = jnp.where(match, gate, weight)
        member = jnp.where(match, 1.0, member)
        matches.append(match)
    left = iota((LINE, LINE), 0)
    right = iota((LINE, LINE), 1)
    ahead = ((left // ROWS == right // ROWS) & (right < left)).astype(F32).astype(BF)
    ranked = jnp.dot(ahead, member.astype(BF), preferred_element_type=F32)
    here = (row // ROWS == (lane % EACH) // CAPACITY) & (
        ranked == (lane % CAPACITY).astype(F32)
    )
    hit = jnp.where(here, member, 0.0)
    return hit, hit * weight, matches


def dispatch_kernel(depth_ref, line_ref, out_ref):
    notes = line_ref[:, 2 * WIDTH :]
    hit, weight, _ = tables(depth_ref[0], notes)
    select = hit.T.astype(BF)
    gates = jnp.sum(weight.T, axis=1, keepdims=True)
    for start in range(0, WIDTH, COLUMNS):
        block = line_ref[:, start : start + COLUMNS]
        out_ref[:, start : start + COLUMNS] = jnp.dot(
            select, block, preferred_element_type=F32
        ).astype(BF)
    for start in range(WIDTH, 2 * WIDTH, COLUMNS):
        block = line_ref[:, start : start + COLUMNS]
        out_ref[:, start : start + COLUMNS] = (
            gates * jnp.dot(select, block, preferred_element_type=F32)
        ).astype(BF)


def dot_t(left, right):
    return lax.dot_general(left, right, (((1,), (1,)), ((), ())), preferred_element_type=F32)


def expert_kernel(rows, gate_hbm, up_hbm, down_hbm, out, gate, up, down, sems):
    copies = [
        pltpu.make_async_copy(gate_hbm, gate, sems.at[0]),
        pltpu.make_async_copy(up_hbm, up, sems.at[1]),
        pltpu.make_async_copy(down_hbm, down, sems.at[2]),
    ]
    for copy in copies:
        copy.start()
    inputs = rows[:, :WIDTH]
    copies[0].wait()
    pre_gate = jnp.dot(inputs, gate[...], preferred_element_type=F32)
    copies[1].wait()
    pre_up = jnp.dot(inputs, up[...], preferred_element_type=F32)
    sigmoid = jax.nn.sigmoid(pre_gate)
    hidden = (pre_gate * sigmoid * pre_up).astype(BF)
    copies[2].wait()
    out[:, :WIDTH] = jnp.dot(hidden, down[...], preferred_element_type=F32).astype(BF)
    grad_hidden = dot_t(rows[:, WIDTH:], down[...])
    grad_gate = (grad_hidden * pre_up * sigmoid * (1.0 + pre_gate * (1.0 - sigmoid))).astype(BF)
    grad_up = (grad_hidden * pre_gate * sigmoid).astype(BF)
    out[:, WIDTH:] = (dot_t(grad_gate, gate[...]) + dot_t(grad_up, up[...])).astype(BF)


def combine_kernel(depth_ref, line_ref, back_ref, out_ref):
    hit, weight, matches = tables(depth_ref[0], line_ref[:, 2 * WIDTH :])
    select = hit.astype(BF)
    high, middle, low = parts_of(weight)
    scores = jnp.zeros((LINE, SLOTS), F32)
    for start in range(0, WIDTH, COLUMNS):
        block = back_ref[:, start : start + COLUMNS]
        mixed = (
            jnp.dot(low, block, preferred_element_type=F32)
            + jnp.dot(middle, block, preferred_element_type=F32)
            + jnp.dot(high, block, preferred_element_type=F32)
        )
        out_ref[:, start : start + COLUMNS] = mixed.astype(BF)
        scores = scores + dot_t(line_ref[:, WIDTH + start : WIDTH + start + COLUMNS], block)
    for start in range(WIDTH, 2 * WIDTH, COLUMNS):
        block = back_ref[:, start : start + COLUMNS]
        out_ref[:, start : start + COLUMNS] = jnp.dot(
            select, block, preferred_element_type=F32
        ).astype(BF)
    scores = jnp.where(hit > 0.0, scores, 0.0)
    lane = iota((LINE, NOTES), 1)
    notes = jnp.zeros((LINE, NOTES), F32)
    for k in range(TOP):
        total = jnp.sum(jnp.where(matches[k], scores, 0.0), axis=1, keepdims=True)
        for part, value in enumerate(parts_of(total)):
            notes = jnp.where(lane == part * TOP + k, value.astype(F32), notes)
    out_ref[:, 2 * WIDTH :] = notes.astype(BF)


def finish_kernel(parts_ref, mixed_ref, rows_ref, gates_ref):
    def total(start, stop):
        value = parts_ref[0, :, start:stop].astype(F32)
        for place in range(1, DEPTH):
            value = value + parts_ref[place, :, start:stop].astype(F32)
        return value

    mixed_ref[...] = total(0, WIDTH).astype(BF)
    rows_ref[...] = total(WIDTH, 2 * WIDTH).astype(BF)
    columns = total(2 * WIDTH, 2 * WIDTH + NOTES).T
    gates_ref[...] = columns[:TOP] + columns[TOP : 2 * TOP] + columns[2 * TOP : 3 * TOP]


def local(tokens, expert_ids, gate_values, w_gate, w_up, w_down, cotangent):
    total = 2 * WIDTH + NOTES
    place = lax.axis_index("expert")
    depth = (lax.axis_index("dp") * EXPERTS + place).astype(jnp.int32).reshape(1)
    spots = [PLANE_STEP * spot % PLANE for spot in range(PLANE)]
    levels = [DEPTH_STEP * level % DEPTH for level in range(DEPTH)]
    planes = [[spot * DEPTH + level for spot in spots] for level in range(DEPTH)]
    lines = [[spot * DEPTH + level for level in levels] for spot in range(PLANE)]

    def at(row, column_high, column_low, level):
        return EXPERTS + (row * 4 + column_high * 2 + column_low) * DEPTH + level

    planes += [
        [at(row, high, low, level) for level in range(DEPTH) for high in range(2)]
        for row in range(4)
        for low in range(2)
    ]
    lines += [
        [at(row, high, low, level) for row in range(4) for low in range(2)]
        for high in range(2)
        for level in range(DEPTH)
    ]

    def exchange(blocks, groups):
        return lax.all_to_all(
            blocks,
            ("dp", "expert"),
            split_axis=0,
            concat_axis=0,
            tiled=True,
            axis_index_groups=groups,
        )

    def near(array):
        return pltpu.with_memory_space_constraint(array, pltpu.VMEM)

    vmem = pl.BlockSpec(memory_space=pltpu.VMEM)
    smem = pl.BlockSpec(memory_space=pltpu.SMEM)
    anywhere = pl.BlockSpec(memory_space=pl.ANY)
    packed = pl.pallas_call(
        pack_kernel,
        out_shape=pltpu.VMEM((LINE, total), BF),
        in_specs=[vmem] * 4,
        out_specs=vmem,
        name="pack",
        compiler_params=pltpu.CompilerParams(vmem_limit_bytes=8 * MIB),
    )(tokens, cotangent, expert_ids.T, gate_values.T)
    line = near(exchange(packed.reshape(DEPTH, ROWS, total), lines).reshape(LINE, total))
    sent = pl.pallas_call(
        dispatch_kernel,
        out_shape=pltpu.VMEM((SLOTS, 2 * WIDTH), BF),
        in_specs=[smem, vmem],
        out_specs=vmem,
        name="dispatch",
        compiler_params=pltpu.CompilerParams(vmem_limit_bytes=16 * MIB),
    )(depth, line)
    received = exchange(sent.reshape(PLANE, EACH, 2 * WIDTH), planes)
    received = near(received.reshape(SLOTS, 2 * WIDTH))
    output = pl.pallas_call(
        expert_kernel,
        out_shape=pltpu.VMEM((SLOTS, 2 * WIDTH), BF),
        in_specs=[vmem, anywhere, anywhere, anywhere],
        out_specs=vmem,
        scratch_shapes=[
            pltpu.VMEM((WIDTH, HIDDEN), BF),
            pltpu.VMEM((WIDTH, HIDDEN), BF),
            pltpu.VMEM((HIDDEN, WIDTH), BF),
            pltpu.SemaphoreType.DMA((3,)),
        ],
        name="expert",
        compiler_params=pltpu.CompilerParams(vmem_limit_bytes=28 * MIB),
    )(received, w_gate[0], w_up[0], w_down[0])
    back = exchange(output.reshape(PLANE, EACH, 2 * WIDTH), planes)
    back = near(back.reshape(SLOTS, 2 * WIDTH))
    parts = pl.pallas_call(
        combine_kernel,
        out_shape=pltpu.VMEM((LINE, total), BF),
        in_specs=[smem, vmem, vmem],
        out_specs=vmem,
        name="combine",
        compiler_params=pltpu.CompilerParams(vmem_limit_bytes=16 * MIB),
    )(depth, line, back)
    parts = near(exchange(parts.reshape(DEPTH, ROWS, total), lines))
    mixed_rows, row_grads, gate_grads = pl.pallas_call(
        finish_kernel,
        out_shape=(
            jax.ShapeDtypeStruct((ROWS, WIDTH), BF),
            jax.ShapeDtypeStruct((ROWS, WIDTH), BF),
            jax.ShapeDtypeStruct((TOP, ROWS), F32),
        ),
        in_specs=[vmem],
        out_specs=(vmem, vmem, vmem),
        name="finish",
        compiler_params=pltpu.CompilerParams(vmem_limit_bytes=8 * MIB),
    )(parts)
    return (mixed_rows, row_grads, gate_grads.T)


def solution(mesh):
    return jax.shard_map(
        local,
        mesh=mesh,
        in_specs=(
            P(("dp", "expert"), None),
            P(("dp", "expert"), None),
            P(("dp", "expert"), None),
            P("expert", None, None),
            P("expert", None, None),
            P("expert", None, None),
            P(("dp", "expert"), None),
        ),
        out_specs=(P(("dp", "expert"), None), P(("dp", "expert"), None), P(("dp", "expert"), None)),
        check_vma=False,
    )
```

```python
import jax
import jax.numpy as jnp
from jax import lax
from jax.experimental import pallas as pl
from jax.experimental.pallas import tpu as pltpu
from jax.sharding import PartitionSpec as P

DEPTH = 8
PLANE = 16
EXPERTS = 128
CAPACITY = 2
PLANE_STEP = 15
DEPTH_STEP = 3
ROWS = 16
TOP = 8
WIDTH = 2048
HIDDEN = 768
NOTES = 128
LINE = DEPTH * ROWS
EACH = DEPTH * CAPACITY
SLOTS = PLANE * EACH
BF = jnp.bfloat16
F32 = jnp.float32
COLUMNS = 512
MIB = 1024 * 1024


def iota(shape, dim):
    return lax.broadcasted_iota(jnp.int32, shape, dim)


def parts_of(values):
    high = values.astype(BF)
    rest = values - high.astype(F32)
    middle = rest.astype(BF)
    low = (rest - middle.astype(F32)).astype(BF)
    return high, middle, low


def pack_kernel(
    tokens_hbm, cotangent_hbm, ids_hbm, gates_hbm, out_ref, tokens, cotangent, ids, gates, sems
):
    copies = [
        pltpu.make_async_copy(ids_hbm, ids, sems.at[0]),
        pltpu.make_async_copy(gates_hbm, gates, sems.at[1]),
        pltpu.make_async_copy(tokens_hbm, tokens, sems.at[2]),
        pltpu.make_async_copy(cotangent_hbm, cotangent, sems.at[3]),
    ]
    for copy in copies:
        copy.start()
    copies[0].wait()
    copies[1].wait()
    high, middle, low = parts_of(gates[...])
    columns = jnp.concatenate(
        [ids[...].astype(F32), high.astype(F32), middle.astype(F32), low.astype(F32)], axis=0
    )
    columns = jnp.concatenate([columns, jnp.zeros((NOTES - 4 * TOP, ROWS), F32)], axis=0)
    notes = columns.T.astype(BF)
    for start in range(0, LINE, ROWS):
        out_ref[start : start + ROWS, 2 * WIDTH :] = notes
    copies[2].wait()
    for start in range(0, LINE, ROWS):
        out_ref[start : start + ROWS, :WIDTH] = tokens[...]
    copies[3].wait()
    for start in range(0, LINE, ROWS):
        out_ref[start : start + ROWS, WIDTH : 2 * WIDTH] = cotangent[...]


def tables(depth, notes):
    notes = notes.astype(F32)
    lane = iota((LINE, SLOTS), 1)
    row = iota((LINE, SLOTS), 0)
    member_of = lane // EACH
    core, place = depth // EXPERTS, depth % EXPERTS
    here = (member_of * PLANE_STEP % PLANE) * DEPTH + place % DEPTH
    other = (place // (2 * DEPTH)) * (2 * DEPTH)
    other = other + (member_of % 2) * DEPTH + member_of // 2
    named = jnp.where(core == 0, here, other).astype(F32)
    matches = []
    weight = jnp.zeros((LINE, SLOTS), F32)
    member = jnp.zeros((LINE, SLOTS), F32)
    for k in range(TOP):
        match = notes[:, k : k + 1] == named
        gate = (
            notes[:, TOP + k : TOP + k + 1]
            + notes[:, 2 * TOP + k : 2 * TOP + k + 1]
            + notes[:, 3 * TOP + k : 3 * TOP + k + 1]
        )
        weight = jnp.where(match, gate, weight)
        member = jnp.where(match, 1.0, member)
        matches.append(match)
    left = iota((LINE, LINE), 0)
    right = iota((LINE, LINE), 1)
    ahead = ((left // ROWS == right // ROWS) & (right < left)).astype(F32).astype(BF)
    ranked = jnp.dot(ahead, member.astype(BF), preferred_element_type=F32)
    here = (row // ROWS == (lane % EACH) // CAPACITY) & (
        ranked == (lane % CAPACITY).astype(F32)
    )
    hit = jnp.where(here, member, 0.0)
    return hit, hit * weight, matches


def dispatch_kernel(depth_ref, line_ref, out_ref):
    notes = line_ref[:, 2 * WIDTH :]
    hit, weight, _ = tables(depth_ref[0], notes)
    select = hit.T.astype(BF)
    gates = jnp.sum(weight.T, axis=1, keepdims=True)
    for start in range(0, WIDTH, COLUMNS):
        block = line_ref[:, start : start + COLUMNS]
        out_ref[:, start : start + COLUMNS] = jnp.dot(
            select, block, preferred_element_type=F32
        ).astype(BF)
    for start in range(WIDTH, 2 * WIDTH, COLUMNS):
        block = line_ref[:, start : start + COLUMNS]
        out_ref[:, start : start + COLUMNS] = (
            gates * jnp.dot(select, block, preferred_element_type=F32)
        ).astype(BF)


def dot_t(left, right):
    return lax.dot_general(left, right, (((1,), (1,)), ((), ())), preferred_element_type=F32)


def expert_kernel(rows, gate, up, down_hbm, out, down, sem):
    copy = pltpu.make_async_copy(down_hbm, down, sem)
    copy.start()
    inputs = rows[:, :WIDTH]
    pre_gate = jnp.dot(inputs, gate[...], preferred_element_type=F32)
    pre_up = jnp.dot(inputs, up[...], preferred_element_type=F32)
    sigmoid = jax.nn.sigmoid(pre_gate)
    hidden = (pre_gate * sigmoid * pre_up).astype(BF)
    copy.wait()
    out[:, :WIDTH] = jnp.dot(hidden, down[...], preferred_element_type=F32).astype(BF)
    grad_hidden = dot_t(rows[:, WIDTH:], down[...])
    grad_gate = (grad_hidden * pre_up * sigmoid * (1.0 + pre_gate * (1.0 - sigmoid))).astype(BF)
    grad_up = (grad_hidden * pre_gate * sigmoid).astype(BF)
    out[:, WIDTH:] = (dot_t(grad_gate, gate[...]) + dot_t(grad_up, up[...])).astype(BF)


def combine_kernel(depth_ref, line_ref, back_ref, out_ref):
    hit, weight, matches = tables(depth_ref[0], line_ref[:, 2 * WIDTH :])
    select = hit.astype(BF)
    high, middle, low = parts_of(weight)
    scores = jnp.zeros((LINE, SLOTS), F32)
    for start in range(0, WIDTH, COLUMNS):
        block = back_ref[:, start : start + COLUMNS]
        mixed = (
            jnp.dot(low, block, preferred_element_type=F32)
            + jnp.dot(middle, block, preferred_element_type=F32)
            + jnp.dot(high, block, preferred_element_type=F32)
        )
        out_ref[:, start : start + COLUMNS] = mixed.astype(BF)
        scores = scores + dot_t(line_ref[:, WIDTH + start : WIDTH + start + COLUMNS], block)
    for start in range(WIDTH, 2 * WIDTH, COLUMNS):
        block = back_ref[:, start : start + COLUMNS]
        out_ref[:, start : start + COLUMNS] = jnp.dot(
            select, block, preferred_element_type=F32
        ).astype(BF)
    scores = jnp.where(hit > 0.0, scores, 0.0)
    lane = iota((LINE, NOTES), 1)
    notes = jnp.zeros((LINE, NOTES), F32)
    for k in range(TOP):
        total = jnp.sum(jnp.where(matches[k], scores, 0.0), axis=1, keepdims=True)
        for part, value in enumerate(parts_of(total)):
            notes = jnp.where(lane == part * TOP + k, value.astype(F32), notes)
    out_ref[:, 2 * WIDTH :] = notes.astype(BF)


def finish_kernel(parts_ref, mixed_ref, rows_ref, gates_ref):
    def total(start, stop):
        value = parts_ref[0, :, start:stop].astype(F32)
        for place in range(1, DEPTH):
            value = value + parts_ref[place, :, start:stop].astype(F32)
        return value

    mixed_ref[...] = total(0, WIDTH).astype(BF)
    rows_ref[...] = total(WIDTH, 2 * WIDTH).astype(BF)
    columns = total(2 * WIDTH, 2 * WIDTH + NOTES).T
    gates_ref[...] = columns[:TOP] + columns[TOP : 2 * TOP] + columns[2 * TOP : 3 * TOP]


def local(tokens, expert_ids, gate_values, w_gate, w_up, w_down, cotangent):
    total = 2 * WIDTH + NOTES
    place = lax.axis_index("expert")
    depth = (lax.axis_index("dp") * EXPERTS + place).astype(jnp.int32).reshape(1)
    spots = [PLANE_STEP * spot % PLANE for spot in range(PLANE)]
    levels = [DEPTH_STEP * level % DEPTH for level in range(DEPTH)]
    planes = [[spot * DEPTH + level for spot in spots] for level in range(DEPTH)]
    lines = [[spot * DEPTH + level for level in levels] for spot in range(PLANE)]

    def at(row, column_high, column_low, level):
        return EXPERTS + (row * 4 + column_high * 2 + column_low) * DEPTH + level

    planes += [
        [at(row, high, low, level) for level in range(DEPTH) for low in range(2)]
        for row in range(4)
        for high in range(2)
    ]
    lines += [
        [at(row, high, low, level) for row in range(4) for high in range(2)]
        for low in range(2)
        for level in range(DEPTH)
    ]

    def exchange(blocks, groups):
        return lax.all_to_all(
            blocks,
            ("dp", "expert"),
            split_axis=0,
            concat_axis=0,
            tiled=True,
            axis_index_groups=groups,
        )

    def near(array):
        return pltpu.with_memory_space_constraint(array, pltpu.VMEM)

    def far(array):
        return pltpu.with_memory_space_constraint(array, pltpu.HBM)

    vmem = pl.BlockSpec(memory_space=pltpu.VMEM)
    smem = pl.BlockSpec(memory_space=pltpu.SMEM)
    anywhere = pl.BlockSpec(memory_space=pl.ANY)
    packed = pl.pallas_call(
        pack_kernel,
        out_shape=pltpu.VMEM((LINE, total), BF),
        in_specs=[anywhere] * 4,
        out_specs=vmem,
        scratch_shapes=[
            pltpu.VMEM((ROWS, WIDTH), BF),
            pltpu.VMEM((ROWS, WIDTH), BF),
            pltpu.VMEM((TOP, ROWS), jnp.int32),
            pltpu.VMEM((TOP, ROWS), F32),
            pltpu.SemaphoreType.DMA((4,)),
        ],
        name="pack",
        compiler_params=pltpu.CompilerParams(vmem_limit_bytes=8 * MIB),
    )(far(tokens), far(cotangent), far(expert_ids.T), far(gate_values.T))
    line = near(exchange(packed.reshape(DEPTH, ROWS, total), lines).reshape(LINE, total))
    sent = pl.pallas_call(
        dispatch_kernel,
        out_shape=pltpu.VMEM((SLOTS, 2 * WIDTH), BF),
        in_specs=[smem, vmem],
        out_specs=vmem,
        name="dispatch",
        compiler_params=pltpu.CompilerParams(vmem_limit_bytes=16 * MIB),
    )(depth, line)
    received = exchange(sent.reshape(PLANE, EACH, 2 * WIDTH), planes)
    received = near(received.reshape(SLOTS, 2 * WIDTH))
    output = pl.pallas_call(
        expert_kernel,
        out_shape=pltpu.VMEM((SLOTS, 2 * WIDTH), BF),
        in_specs=[vmem, vmem, vmem, anywhere],
        out_specs=vmem,
        scratch_shapes=[
            pltpu.VMEM((HIDDEN, WIDTH), BF),
            pltpu.SemaphoreType.DMA,
        ],
        name="expert",
        compiler_params=pltpu.CompilerParams(vmem_limit_bytes=28 * MIB),
    )(received, near(w_gate[0]), near(w_up[0]), far(w_down[0]))
    back = exchange(output.reshape(PLANE, EACH, 2 * WIDTH), planes)
    back = near(back.reshape(SLOTS, 2 * WIDTH))
    parts = pl.pallas_call(
        combine_kernel,
        out_shape=pltpu.VMEM((LINE, total), BF),
        in_specs=[smem, vmem, vmem],
        out_specs=vmem,
        name="combine",
        compiler_params=pltpu.CompilerParams(vmem_limit_bytes=16 * MIB),
    )(depth, line, back)
    parts = near(exchange(parts.reshape(DEPTH, ROWS, total), lines))
    mixed_rows, row_grads, gate_grads = pl.pallas_call(
        finish_kernel,
        out_shape=(
            jax.ShapeDtypeStruct((ROWS, WIDTH), BF),
            jax.ShapeDtypeStruct((ROWS, WIDTH), BF),
            jax.ShapeDtypeStruct((TOP, ROWS), F32),
        ),
        in_specs=[vmem],
        out_specs=(vmem, vmem, vmem),
        name="finish",
        compiler_params=pltpu.CompilerParams(vmem_limit_bytes=8 * MIB),
    )(parts)
    return (mixed_rows, row_grads, gate_grads.T)


def solution(mesh):
    return jax.shard_map(
        local,
        mesh=mesh,
        in_specs=(
            P(("dp", "expert"), None),
            P(("dp", "expert"), None),
            P(("dp", "expert"), None),
            P("expert", None, None),
            P("expert", None, None),
            P("expert", None, None),
            P(("dp", "expert"), None),
        ),
        out_specs=(P(("dp", "expert"), None), P(("dp", "expert"), None), P(("dp", "expert"), None)),
        check_vma=False,
    )
```

```python
import jax
import jax.numpy as jnp
from jax import lax
from jax.experimental import pallas as pl
from jax.experimental.pallas import tpu as pltpu
from jax.sharding import PartitionSpec as P

DEPTH = 8
PLANE = 16
EXPERTS = 128
CAPACITY = 2
PLANE_STEP = 7
DEPTH_STEP = 3
ROWS = 16
TOP = 8
WIDTH = 2048
HIDDEN = 768
NOTES = 128
LINE = DEPTH * ROWS
EACH = DEPTH * CAPACITY
SLOTS = PLANE * EACH
BF = jnp.bfloat16
F32 = jnp.float32
COLUMNS = 512
STAGGER = 17500
MIB = 1024 * 1024


def iota(shape, dim):
    return lax.broadcasted_iota(jnp.int32, shape, dim)


def parts_of(values):
    high = values.astype(BF)
    rest = values - high.astype(F32)
    middle = rest.astype(BF)
    low = (rest - middle.astype(F32)).astype(BF)
    return high, middle, low


def pack_kernel(
    depth_ref, tokens_hbm, cotangent_hbm, ids_hbm, gates_hbm, out_ref, tokens, cotangent, ids, gates, sems
):
    copies = [
        pltpu.make_async_copy(ids_hbm, ids, sems.at[0]),
        pltpu.make_async_copy(gates_hbm, gates, sems.at[1]),
        pltpu.make_async_copy(tokens_hbm, tokens, sems.at[2]),
        pltpu.make_async_copy(cotangent_hbm, cotangent, sems.at[3]),
    ]
    for copy in copies:
        copy.start()

    @pl.when(depth_ref[0] >= EXPERTS)
    def _():
        pl.delay(STAGGER)

    copies[0].wait()
    copies[1].wait()
    high, middle, low = parts_of(gates[...])
    columns = jnp.concatenate(
        [ids[...].astype(F32), high.astype(F32), middle.astype(F32), low.astype(F32)], axis=0
    )
    columns = jnp.concatenate([columns, jnp.zeros((NOTES - 4 * TOP, ROWS), F32)], axis=0)
    notes = columns.T.astype(BF)
    for start in range(0, LINE, ROWS):
        out_ref[start : start + ROWS, 2 * WIDTH :] = notes
    copies[2].wait()
    for start in range(0, LINE, ROWS):
        out_ref[start : start + ROWS, :WIDTH] = tokens[...]
    copies[3].wait()
    for start in range(0, LINE, ROWS):
        out_ref[start : start + ROWS, WIDTH : 2 * WIDTH] = cotangent[...]


def tables(depth, notes):
    notes = notes.astype(F32)
    lane = iota((LINE, SLOTS), 1)
    row = iota((LINE, SLOTS), 0)
    member_of = lane // EACH
    place = depth % EXPERTS
    named = ((member_of * PLANE_STEP % PLANE) * DEPTH + place % DEPTH).astype(F32)
    matches = []
    weight = jnp.zeros((LINE, SLOTS), F32)
    member = jnp.zeros((LINE, SLOTS), F32)
    for k in range(TOP):
        match = notes[:, k : k + 1] == named
        gate = (
            notes[:, TOP + k : TOP + k + 1]
            + notes[:, 2 * TOP + k : 2 * TOP + k + 1]
            + notes[:, 3 * TOP + k : 3 * TOP + k + 1]
        )
        weight = jnp.where(match, gate, weight)
        member = jnp.where(match, 1.0, member)
        matches.append(match)
    left = iota((LINE, LINE), 0)
    right = iota((LINE, LINE), 1)
    ahead = ((left // ROWS == right // ROWS) & (right < left)).astype(F32).astype(BF)
    ranked = jnp.dot(ahead, member.astype(BF), preferred_element_type=F32)
    here = (row // ROWS == (lane % EACH) // CAPACITY) & (
        ranked == (lane % CAPACITY).astype(F32)
    )
    hit = jnp.where(here, member, 0.0)
    return hit, hit * weight, matches


def dispatch_kernel(depth_ref, line_ref, out_ref):
    notes = line_ref[:, 2 * WIDTH :]
    hit, weight, _ = tables(depth_ref[0], notes)
    select = hit.T.astype(BF)
    gates = jnp.sum(weight.T, axis=1, keepdims=True)
    for start in range(0, WIDTH, COLUMNS):
        block = line_ref[:, start : start + COLUMNS]
        out_ref[:, start : start + COLUMNS] = jnp.dot(
            select, block, preferred_element_type=F32
        ).astype(BF)
    for start in range(WIDTH, 2 * WIDTH, COLUMNS):
        block = line_ref[:, start : start + COLUMNS]
        out_ref[:, start : start + COLUMNS] = (
            gates * jnp.dot(select, block, preferred_element_type=F32)
        ).astype(BF)


def dot_t(left, right):
    return lax.dot_general(left, right, (((1,), (1,)), ((), ())), preferred_element_type=F32)


def expert_kernel(rows, gate, up, down_hbm, out, down, sem):
    copy = pltpu.make_async_copy(down_hbm, down, sem)
    copy.start()
    inputs = rows[:, :WIDTH]
    pre_gate = jnp.dot(inputs, gate[...], preferred_element_type=F32)
    pre_up = jnp.dot(inputs, up[...], preferred_element_type=F32)
    sigmoid = jax.nn.sigmoid(pre_gate)
    hidden = (pre_gate * sigmoid * pre_up).astype(BF)
    copy.wait()
    out[:, :WIDTH] = jnp.dot(hidden, down[...], preferred_element_type=F32).astype(BF)
    grad_hidden = dot_t(rows[:, WIDTH:], down[...])
    grad_gate = (grad_hidden * pre_up * sigmoid * (1.0 + pre_gate * (1.0 - sigmoid))).astype(BF)
    grad_up = (grad_hidden * pre_gate * sigmoid).astype(BF)
    out[:, WIDTH:] = (dot_t(grad_gate, gate[...]) + dot_t(grad_up, up[...])).astype(BF)


def combine_kernel(depth_ref, line_ref, back_ref, out_ref):
    hit, weight, matches = tables(depth_ref[0], line_ref[:, 2 * WIDTH :])
    select = hit.astype(BF)
    high, middle, low = parts_of(weight)
    scores = jnp.zeros((LINE, SLOTS), F32)
    for start in range(0, WIDTH, COLUMNS):
        block = back_ref[:, start : start + COLUMNS]
        mixed = (
            jnp.dot(low, block, preferred_element_type=F32)
            + jnp.dot(middle, block, preferred_element_type=F32)
            + jnp.dot(high, block, preferred_element_type=F32)
        )
        out_ref[:, start : start + COLUMNS] = mixed.astype(BF)
        scores = scores + dot_t(line_ref[:, WIDTH + start : WIDTH + start + COLUMNS], block)
    for start in range(WIDTH, 2 * WIDTH, COLUMNS):
        block = back_ref[:, start : start + COLUMNS]
        out_ref[:, start : start + COLUMNS] = jnp.dot(
            select, block, preferred_element_type=F32
        ).astype(BF)
    scores = jnp.where(hit > 0.0, scores, 0.0)
    lane = iota((LINE, NOTES), 1)
    notes = jnp.zeros((LINE, NOTES), F32)
    for k in range(TOP):
        total = jnp.sum(jnp.where(matches[k], scores, 0.0), axis=1, keepdims=True)
        for part, value in enumerate(parts_of(total)):
            notes = jnp.where(lane == part * TOP + k, value.astype(F32), notes)
    out_ref[:, 2 * WIDTH :] = notes.astype(BF)


def finish_kernel(parts_ref, mixed_ref, rows_ref, gates_ref):
    def total(start, stop):
        value = parts_ref[0, :, start:stop].astype(F32)
        for place in range(1, DEPTH):
            value = value + parts_ref[place, :, start:stop].astype(F32)
        return value

    mixed_ref[...] = total(0, WIDTH).astype(BF)
    rows_ref[...] = total(WIDTH, 2 * WIDTH).astype(BF)
    columns = total(2 * WIDTH, 2 * WIDTH + NOTES).T
    gates_ref[...] = columns[:TOP] + columns[TOP : 2 * TOP] + columns[2 * TOP : 3 * TOP]


def local(tokens, expert_ids, gate_values, w_gate, w_up, w_down, cotangent):
    total = 2 * WIDTH + NOTES
    place = lax.axis_index("expert")
    depth = (lax.axis_index("dp") * EXPERTS + place).astype(jnp.int32).reshape(1)
    spots = [PLANE_STEP * spot % PLANE for spot in range(PLANE)]
    levels = [DEPTH_STEP * level % DEPTH for level in range(DEPTH)]
    planes = [[spot * DEPTH + level for spot in spots] for level in range(DEPTH)]
    lines = [[spot * DEPTH + level for level in levels] for spot in range(PLANE)]

    planes += [[EXPERTS + member for member in group] for group in planes]
    lines += [[EXPERTS + member for member in group] for group in lines]

    def exchange(blocks, groups):
        return lax.all_to_all(
            blocks,
            ("dp", "expert"),
            split_axis=0,
            concat_axis=0,
            tiled=True,
            axis_index_groups=groups,
        )

    def near(array):
        return pltpu.with_memory_space_constraint(array, pltpu.VMEM)

    def far(array):
        return pltpu.with_memory_space_constraint(array, pltpu.HBM)

    vmem = pl.BlockSpec(memory_space=pltpu.VMEM)
    smem = pl.BlockSpec(memory_space=pltpu.SMEM)
    anywhere = pl.BlockSpec(memory_space=pl.ANY)
    packed = pl.pallas_call(
        pack_kernel,
        out_shape=pltpu.VMEM((LINE, total), BF),
        in_specs=[smem] + [anywhere] * 4,
        out_specs=vmem,
        scratch_shapes=[
            pltpu.VMEM((ROWS, WIDTH), BF),
            pltpu.VMEM((ROWS, WIDTH), BF),
            pltpu.VMEM((TOP, ROWS), jnp.int32),
            pltpu.VMEM((TOP, ROWS), F32),
            pltpu.SemaphoreType.DMA((4,)),
        ],
        name="pack",
        compiler_params=pltpu.CompilerParams(vmem_limit_bytes=8 * MIB),
    )(depth, far(tokens), far(cotangent), far(expert_ids.T), far(gate_values.T))
    line = near(exchange(packed.reshape(DEPTH, ROWS, total), lines).reshape(LINE, total))
    sent = pl.pallas_call(
        dispatch_kernel,
        out_shape=pltpu.VMEM((SLOTS, 2 * WIDTH), BF),
        in_specs=[smem, vmem],
        out_specs=vmem,
        name="dispatch",
        compiler_params=pltpu.CompilerParams(vmem_limit_bytes=16 * MIB),
    )(depth, line)
    received = exchange(sent.reshape(PLANE, EACH, 2 * WIDTH), planes)
    received = near(received.reshape(SLOTS, 2 * WIDTH))
    output = pl.pallas_call(
        expert_kernel,
        out_shape=pltpu.VMEM((SLOTS, 2 * WIDTH), BF),
        in_specs=[vmem, vmem, vmem, anywhere],
        out_specs=vmem,
        scratch_shapes=[
            pltpu.VMEM((HIDDEN, WIDTH), BF),
            pltpu.SemaphoreType.DMA,
        ],
        name="expert",
        compiler_params=pltpu.CompilerParams(vmem_limit_bytes=28 * MIB),
    )(received, near(w_gate[0]), near(w_up[0]), far(w_down[0]))
    back = exchange(output.reshape(PLANE, EACH, 2 * WIDTH), planes)
    back = near(back.reshape(SLOTS, 2 * WIDTH))
    parts = pl.pallas_call(
        combine_kernel,
        out_shape=pltpu.VMEM((LINE, total), BF),
        in_specs=[smem, vmem, vmem],
        out_specs=vmem,
        name="combine",
        compiler_params=pltpu.CompilerParams(vmem_limit_bytes=16 * MIB),
    )(depth, line, back)
    parts = near(exchange(parts.reshape(DEPTH, ROWS, total), lines))
    mixed_rows, row_grads, gate_grads = pl.pallas_call(
        finish_kernel,
        out_shape=(
            jax.ShapeDtypeStruct((ROWS, WIDTH), BF),
            jax.ShapeDtypeStruct((ROWS, WIDTH), BF),
            jax.ShapeDtypeStruct((TOP, ROWS), F32),
        ),
        in_specs=[vmem],
        out_specs=(vmem, vmem, vmem),
        name="finish",
        compiler_params=pltpu.CompilerParams(vmem_limit_bytes=8 * MIB),
    )(parts)
    return (mixed_rows, row_grads, gate_grads.T)


def solution(mesh):
    return jax.shard_map(
        local,
        mesh=mesh,
        in_specs=(
            P(("dp", "expert"), None),
            P(("dp", "expert"), None),
            P(("dp", "expert"), None),
            P("expert", None, None),
            P("expert", None, None),
            P("expert", None, None),
            P(("dp", "expert"), None),
        ),
        out_specs=(P(("dp", "expert"), None), P(("dp", "expert"), None), P(("dp", "expert"), None)),
        check_vma=False,
    )
```

```python
import jax
import jax.numpy as jnp
from jax import lax
from jax.experimental import pallas as pl
from jax.experimental.pallas import tpu as pltpu
from jax.sharding import PartitionSpec as P

DEPTH = 8
PLANE = 16
EXPERTS = 128
CAPACITY = 2
PLANE_STEP = 7
DEPTH_STEP = 3
ROWS = 16
TOP = 8
WIDTH = 2048
HIDDEN = 768
NOTES = 128
LINE = DEPTH * ROWS
EACH = DEPTH * CAPACITY
SLOTS = PLANE * EACH
BF = jnp.bfloat16
F32 = jnp.float32
COLUMNS = 512
STAGGER = 17500
MIB = 1024 * 1024


def iota(shape, dim):
    return lax.broadcasted_iota(jnp.int32, shape, dim)


def parts_of(values):
    high = values.astype(BF)
    rest = values - high.astype(F32)
    middle = rest.astype(BF)
    low = (rest - middle.astype(F32)).astype(BF)
    return high, middle, low


def pack_kernel(
    depth_ref, tokens_hbm, cotangent_hbm, ids_hbm, gates_hbm, out_ref, tokens, cotangent, ids, gates, sems
):
    copies = [
        pltpu.make_async_copy(ids_hbm, ids, sems.at[0]),
        pltpu.make_async_copy(gates_hbm, gates, sems.at[1]),
        pltpu.make_async_copy(tokens_hbm, tokens, sems.at[2]),
        pltpu.make_async_copy(cotangent_hbm, cotangent, sems.at[3]),
    ]
    for copy in copies:
        copy.start()

    @pl.when(depth_ref[0] >= EXPERTS)
    def _():
        pl.delay(STAGGER)

    copies[0].wait()
    copies[1].wait()
    high, middle, low = parts_of(gates[...])
    columns = jnp.concatenate(
        [ids[...].astype(F32), high.astype(F32), middle.astype(F32), low.astype(F32)], axis=0
    )
    columns = jnp.concatenate([columns, jnp.zeros((NOTES - 4 * TOP, ROWS), F32)], axis=0)
    notes = columns.T.astype(BF)
    for start in range(0, LINE, ROWS):
        out_ref[start : start + ROWS, 2 * WIDTH :] = notes
    copies[2].wait()
    for start in range(0, LINE, ROWS):
        out_ref[start : start + ROWS, :WIDTH] = tokens[...]
    copies[3].wait()
    for start in range(0, LINE, ROWS):
        out_ref[start : start + ROWS, WIDTH : 2 * WIDTH] = cotangent[...]


def tables(depth, notes):
    notes = notes.astype(F32)
    lane = iota((LINE, SLOTS), 1)
    row = iota((LINE, SLOTS), 0)
    member_of = lane // EACH
    place = depth % EXPERTS
    named = ((member_of * PLANE_STEP % PLANE) * DEPTH + place % DEPTH).astype(F32)
    weight = jnp.zeros((LINE, SLOTS), F32)
    pick = jnp.full((LINE, SLOTS), -1.0, F32)
    for k in range(TOP):
        match = notes[:, k : k + 1] == named
        gate = (
            notes[:, TOP + k : TOP + k + 1]
            + notes[:, 2 * TOP + k : 2 * TOP + k + 1]
            + notes[:, 3 * TOP + k : 3 * TOP + k + 1]
        )
        weight = jnp.where(match, gate, weight)
        pick = jnp.where(match, float(k), pick)
    member = jnp.where(pick >= 0.0, 1.0, 0.0)
    left = iota((LINE, LINE), 0)
    right = iota((LINE, LINE), 1)
    ahead = ((left // ROWS == right // ROWS) & (right < left)).astype(F32).astype(BF)
    ranked = jnp.dot(ahead, member.astype(BF), preferred_element_type=F32)
    here = (row // ROWS == (lane % EACH) // CAPACITY) & (
        ranked == (lane % CAPACITY).astype(F32)
    )
    hit = jnp.where(here, member, 0.0)
    return hit, hit * weight, jnp.where(hit > 0.0, pick, -1.0)


def dispatch_kernel(depth_ref, line_ref, out_ref, weight_ref, pick_ref):
    notes = line_ref[:, 2 * WIDTH :]
    hit, weight, pick = tables(depth_ref[0], notes)
    weight_ref[...] = weight
    pick_ref[...] = pick
    select = hit.T.astype(BF)
    gates = jnp.sum(weight.T, axis=1, keepdims=True)
    for start in range(0, WIDTH, COLUMNS):
        block = line_ref[:, start : start + COLUMNS]
        out_ref[:, start : start + COLUMNS] = jnp.dot(
            select, block, preferred_element_type=F32
        ).astype(BF)
    for start in range(WIDTH, 2 * WIDTH, COLUMNS):
        block = line_ref[:, start : start + COLUMNS]
        out_ref[:, start : start + COLUMNS] = (
            gates * jnp.dot(select, block, preferred_element_type=F32)
        ).astype(BF)


def dot_t(left, right):
    return lax.dot_general(left, right, (((1,), (1,)), ((), ())), preferred_element_type=F32)


def expert_kernel(rows, gate, up, down_hbm, out, down, sem):
    copy = pltpu.make_async_copy(down_hbm, down, sem)
    copy.start()
    inputs = rows[:, :WIDTH]
    pre_gate = jnp.dot(inputs, gate[...], preferred_element_type=F32)
    pre_up = jnp.dot(inputs, up[...], preferred_element_type=F32)
    sigmoid = jax.nn.sigmoid(pre_gate)
    hidden = (pre_gate * sigmoid * pre_up).astype(BF)
    copy.wait()
    out[:, :WIDTH] = jnp.dot(hidden, down[...], preferred_element_type=F32).astype(BF)
    grad_hidden = dot_t(rows[:, WIDTH:], down[...])
    grad_gate = (grad_hidden * pre_up * sigmoid * (1.0 + pre_gate * (1.0 - sigmoid))).astype(BF)
    grad_up = (grad_hidden * pre_gate * sigmoid).astype(BF)
    out[:, WIDTH:] = (dot_t(grad_gate, gate[...]) + dot_t(grad_up, up[...])).astype(BF)


def combine_kernel(weight_ref, pick_ref, line_ref, back_ref, out_ref):
    pick = pick_ref[...]
    select = jnp.where(pick >= 0.0, 1.0, 0.0).astype(BF)
    high, middle, low = parts_of(weight_ref[...])
    scores = jnp.zeros((LINE, SLOTS), F32)
    for start in range(0, WIDTH, COLUMNS):
        block = back_ref[:, start : start + COLUMNS]
        mixed = (
            jnp.dot(low, block, preferred_element_type=F32)
            + jnp.dot(middle, block, preferred_element_type=F32)
            + jnp.dot(high, block, preferred_element_type=F32)
        )
        out_ref[:, start : start + COLUMNS] = mixed.astype(BF)
        scores = scores + dot_t(line_ref[:, WIDTH + start : WIDTH + start + COLUMNS], block)
    for start in range(WIDTH, 2 * WIDTH, COLUMNS):
        block = back_ref[:, start : start + COLUMNS]
        out_ref[:, start : start + COLUMNS] = jnp.dot(
            select, block, preferred_element_type=F32
        ).astype(BF)
    lane = iota((LINE, NOTES), 1)
    notes = jnp.zeros((LINE, NOTES), F32)
    for k in range(TOP):
        total = jnp.sum(jnp.where(pick == float(k), scores, 0.0), axis=1, keepdims=True)
        for part, value in enumerate(parts_of(total)):
            notes = jnp.where(lane == part * TOP + k, value.astype(F32), notes)
    out_ref[:, 2 * WIDTH :] = notes.astype(BF)


def finish_kernel(parts_ref, mixed_ref, rows_ref, gates_ref):
    def total(start, stop):
        value = parts_ref[0, :, start:stop].astype(F32)
        for place in range(1, DEPTH):
            value = value + parts_ref[place, :, start:stop].astype(F32)
        return value

    mixed_ref[...] = total(0, WIDTH).astype(BF)
    rows_ref[...] = total(WIDTH, 2 * WIDTH).astype(BF)
    columns = total(2 * WIDTH, 2 * WIDTH + NOTES).T
    gates_ref[...] = columns[:TOP] + columns[TOP : 2 * TOP] + columns[2 * TOP : 3 * TOP]


def local(tokens, expert_ids, gate_values, w_gate, w_up, w_down, cotangent):
    total = 2 * WIDTH + NOTES
    place = lax.axis_index("expert")
    depth = (lax.axis_index("dp") * EXPERTS + place).astype(jnp.int32).reshape(1)
    spots = [PLANE_STEP * spot % PLANE for spot in range(PLANE)]
    levels = [DEPTH_STEP * level % DEPTH for level in range(DEPTH)]
    planes = [[spot * DEPTH + level for spot in spots] for level in range(DEPTH)]
    lines = [[spot * DEPTH + level for level in levels] for spot in range(PLANE)]

    planes += [[EXPERTS + member for member in group] for group in planes]
    lines += [[EXPERTS + member for member in group] for group in lines]

    def exchange(blocks, groups):
        return lax.all_to_all(
            blocks,
            ("dp", "expert"),
            split_axis=0,
            concat_axis=0,
            tiled=True,
            axis_index_groups=groups,
        )

    def near(array):
        return pltpu.with_memory_space_constraint(array, pltpu.VMEM)

    def far(array):
        return pltpu.with_memory_space_constraint(array, pltpu.HBM)

    vmem = pl.BlockSpec(memory_space=pltpu.VMEM)
    smem = pl.BlockSpec(memory_space=pltpu.SMEM)
    anywhere = pl.BlockSpec(memory_space=pl.ANY)
    packed = pl.pallas_call(
        pack_kernel,
        out_shape=pltpu.VMEM((LINE, total), BF),
        in_specs=[smem] + [anywhere] * 4,
        out_specs=vmem,
        scratch_shapes=[
            pltpu.VMEM((ROWS, WIDTH), BF),
            pltpu.VMEM((ROWS, WIDTH), BF),
            pltpu.VMEM((TOP, ROWS), jnp.int32),
            pltpu.VMEM((TOP, ROWS), F32),
            pltpu.SemaphoreType.DMA((4,)),
        ],
        name="pack",
        compiler_params=pltpu.CompilerParams(vmem_limit_bytes=8 * MIB),
    )(depth, far(tokens), far(cotangent), far(expert_ids.T), far(gate_values.T))
    line = near(exchange(packed.reshape(DEPTH, ROWS, total), lines).reshape(LINE, total))
    sent, weight, pick = pl.pallas_call(
        dispatch_kernel,
        out_shape=(
            pltpu.VMEM((SLOTS, 2 * WIDTH), BF),
            pltpu.VMEM((LINE, SLOTS), F32),
            pltpu.VMEM((LINE, SLOTS), F32),
        ),
        in_specs=[smem, vmem],
        out_specs=(vmem, vmem, vmem),
        name="dispatch",
        compiler_params=pltpu.CompilerParams(vmem_limit_bytes=16 * MIB),
    )(depth, line)
    received = exchange(sent.reshape(PLANE, EACH, 2 * WIDTH), planes)
    received = near(received.reshape(SLOTS, 2 * WIDTH))
    output = pl.pallas_call(
        expert_kernel,
        out_shape=pltpu.VMEM((SLOTS, 2 * WIDTH), BF),
        in_specs=[vmem, vmem, vmem, anywhere],
        out_specs=vmem,
        scratch_shapes=[
            pltpu.VMEM((HIDDEN, WIDTH), BF),
            pltpu.SemaphoreType.DMA,
        ],
        name="expert",
        compiler_params=pltpu.CompilerParams(vmem_limit_bytes=28 * MIB),
    )(received, near(w_gate[0]), near(w_up[0]), far(w_down[0]))
    back = exchange(output.reshape(PLANE, EACH, 2 * WIDTH), planes)
    back = near(back.reshape(SLOTS, 2 * WIDTH))
    parts = pl.pallas_call(
        combine_kernel,
        out_shape=pltpu.VMEM((LINE, total), BF),
        in_specs=[vmem] * 4,
        out_specs=vmem,
        name="combine",
        compiler_params=pltpu.CompilerParams(vmem_limit_bytes=16 * MIB),
    )(near(weight), near(pick), line, back)
    parts = near(exchange(parts.reshape(DEPTH, ROWS, total), lines))
    mixed_rows, row_grads, gate_grads = pl.pallas_call(
        finish_kernel,
        out_shape=(
            jax.ShapeDtypeStruct((ROWS, WIDTH), BF),
            jax.ShapeDtypeStruct((ROWS, WIDTH), BF),
            jax.ShapeDtypeStruct((TOP, ROWS), F32),
        ),
        in_specs=[vmem],
        out_specs=(vmem, vmem, vmem),
        name="finish",
        compiler_params=pltpu.CompilerParams(vmem_limit_bytes=8 * MIB),
    )(parts)
    return (mixed_rows, row_grads, gate_grads.T)


def solution(mesh):
    return jax.shard_map(
        local,
        mesh=mesh,
        in_specs=(
            P(("dp", "expert"), None),
            P(("dp", "expert"), None),
            P(("dp", "expert"), None),
            P("expert", None, None),
            P("expert", None, None),
            P("expert", None, None),
            P(("dp", "expert"), None),
        ),
        out_specs=(P(("dp", "expert"), None), P(("dp", "expert"), None), P(("dp", "expert"), None)),
        check_vma=False,
    )
```

```python
import jax
import jax.numpy as jnp
from jax import lax
from jax.experimental import pallas as pl
from jax.experimental.pallas import tpu as pltpu
from jax.sharding import PartitionSpec as P

DEPTH = 8
PLANE = 16
EXPERTS = 128
CAPACITY = 2
PLANE_STEP = 7
DEPTH_STEP = 3
ROWS = 16
TOP = 8
WIDTH = 2048
HIDDEN = 768
NOTES = 128
LINE = DEPTH * ROWS
EACH = DEPTH * CAPACITY
SLOTS = PLANE * EACH
BF = jnp.bfloat16
F32 = jnp.float32
COLUMNS = 512
STAGGER = 17000
MIB = 1024 * 1024


def iota(shape, dim):
    return lax.broadcasted_iota(jnp.int32, shape, dim)


def parts_of(values):
    high = values.astype(BF)
    rest = values - high.astype(F32)
    middle = rest.astype(BF)
    low = (rest - middle.astype(F32)).astype(BF)
    return high, middle, low


def pack_kernel(
    depth_ref, tokens_hbm, cotangent_hbm, ids_hbm, gates_hbm, out_ref, tokens, cotangent, ids, gates, sems
):
    copies = [
        pltpu.make_async_copy(ids_hbm, ids, sems.at[0]),
        pltpu.make_async_copy(gates_hbm, gates, sems.at[1]),
        pltpu.make_async_copy(tokens_hbm, tokens, sems.at[2]),
        pltpu.make_async_copy(cotangent_hbm, cotangent, sems.at[3]),
    ]
    for copy in copies:
        copy.start()

    @pl.when(depth_ref[0] >= EXPERTS)
    def _():
        pl.delay(STAGGER)

    copies[0].wait()
    copies[1].wait()
    high, middle, low = parts_of(gates[...])
    columns = jnp.concatenate(
        [ids[...].astype(F32), high.astype(F32), middle.astype(F32), low.astype(F32)], axis=0
    )
    columns = jnp.concatenate([columns, jnp.zeros((NOTES - 4 * TOP, ROWS), F32)], axis=0)
    notes = columns.T.astype(BF)
    for start in range(0, LINE, ROWS):
        out_ref[start : start + ROWS, 2 * WIDTH :] = notes
    copies[2].wait()
    for start in range(0, LINE, ROWS):
        out_ref[start : start + ROWS, :WIDTH] = tokens[...]
    copies[3].wait()
    for start in range(0, LINE, ROWS):
        out_ref[start : start + ROWS, WIDTH : 2 * WIDTH] = cotangent[...]


def tables(depth, notes):
    notes = notes.astype(F32)
    lane = iota((LINE, SLOTS), 1)
    row = iota((LINE, SLOTS), 0)
    member_of = lane // EACH
    place = depth % EXPERTS
    named = ((member_of * PLANE_STEP % PLANE) * DEPTH + place % DEPTH).astype(F32)
    weight = jnp.zeros((LINE, SLOTS), F32)
    pick = jnp.full((LINE, SLOTS), -1.0, F32)
    for k in range(TOP):
        match = notes[:, k : k + 1] == named
        gate = (
            notes[:, TOP + k : TOP + k + 1]
            + notes[:, 2 * TOP + k : 2 * TOP + k + 1]
            + notes[:, 3 * TOP + k : 3 * TOP + k + 1]
        )
        weight = jnp.where(match, gate, weight)
        pick = jnp.where(match, float(k), pick)
    member = jnp.where(pick >= 0.0, 1.0, 0.0)
    left = iota((LINE, LINE), 0)
    right = iota((LINE, LINE), 1)
    ahead = ((left // ROWS == right // ROWS) & (right < left)).astype(F32).astype(BF)
    ranked = jnp.dot(ahead, member.astype(BF), preferred_element_type=F32)
    here = (row // ROWS == (lane % EACH) // CAPACITY) & (
        ranked == (lane % CAPACITY).astype(F32)
    )
    hit = jnp.where(here, member, 0.0)
    return hit, hit * weight, jnp.where(hit > 0.0, pick, -1.0)


def dispatch_kernel(depth_ref, line_ref, out_ref, weight_ref, pick_ref):
    notes = line_ref[:, 2 * WIDTH :]
    hit, weight, pick = tables(depth_ref[0], notes)
    weight_ref[...] = weight
    pick_ref[...] = pick
    select = hit.T.astype(BF)
    gates = jnp.sum(weight.T, axis=1, keepdims=True)
    for start in range(0, WIDTH, COLUMNS):
        block = line_ref[:, start : start + COLUMNS]
        out_ref[:, start : start + COLUMNS] = jnp.dot(
            select, block, preferred_element_type=F32
        ).astype(BF)
    for start in range(WIDTH, 2 * WIDTH, COLUMNS):
        block = line_ref[:, start : start + COLUMNS]
        out_ref[:, start : start + COLUMNS] = (
            gates * jnp.dot(select, block, preferred_element_type=F32)
        ).astype(BF)


def dot_t(left, right):
    return lax.dot_general(left, right, (((1,), (1,)), ((), ())), preferred_element_type=F32)


def expert_kernel(rows, gate, up, down_hbm, out, down, sem):
    copy = pltpu.make_async_copy(down_hbm, down, sem)
    copy.start()
    inputs = rows[:, :WIDTH]
    pre_gate = jnp.dot(inputs, gate[...], preferred_element_type=F32)
    pre_up = jnp.dot(inputs, up[...], preferred_element_type=F32)
    sigmoid = jax.nn.sigmoid(pre_gate)
    hidden = (pre_gate * sigmoid * pre_up).astype(BF)
    copy.wait()
    out[:, :WIDTH] = jnp.dot(hidden, down[...], preferred_element_type=F32).astype(BF)
    grad_hidden = dot_t(rows[:, WIDTH:], down[...])
    grad_gate = (grad_hidden * pre_up * sigmoid * (1.0 + pre_gate * (1.0 - sigmoid))).astype(BF)
    grad_up = (grad_hidden * pre_gate * sigmoid).astype(BF)
    out[:, WIDTH:] = (dot_t(grad_gate, gate[...]) + dot_t(grad_up, up[...])).astype(BF)


def combine_kernel(weight_ref, pick_ref, line_ref, back_ref, out_ref):
    pick = pick_ref[...]
    select = jnp.where(pick >= 0.0, 1.0, 0.0).astype(BF)
    high, middle, low = parts_of(weight_ref[...])
    scores = jnp.zeros((LINE, SLOTS), F32)
    for start in range(0, WIDTH, COLUMNS):
        block = back_ref[:, start : start + COLUMNS]
        mixed = (
            jnp.dot(low, block, preferred_element_type=F32)
            + jnp.dot(middle, block, preferred_element_type=F32)
            + jnp.dot(high, block, preferred_element_type=F32)
        )
        out_ref[:, start : start + COLUMNS] = mixed.astype(BF)
        scores = scores + dot_t(line_ref[:, WIDTH + start : WIDTH + start + COLUMNS], block)
    for start in range(WIDTH, 2 * WIDTH, COLUMNS):
        block = back_ref[:, start : start + COLUMNS]
        out_ref[:, start : start + COLUMNS] = jnp.dot(
            select, block, preferred_element_type=F32
        ).astype(BF)
    lane = iota((LINE, NOTES), 1)
    notes = jnp.zeros((LINE, NOTES), F32)
    for k in range(TOP):
        total = jnp.sum(jnp.where(pick == float(k), scores, 0.0), axis=1, keepdims=True)
        for part, value in enumerate(parts_of(total)):
            notes = jnp.where(lane == part * TOP + k, value.astype(F32), notes)
    out_ref[:, 2 * WIDTH :] = notes.astype(BF)


def finish_kernel(parts_ref, mixed_ref, rows_ref, gates_ref):
    def total(start, stop):
        value = parts_ref[0, :, start:stop].astype(F32)
        for place in range(1, DEPTH):
            value = value + parts_ref[place, :, start:stop].astype(F32)
        return value

    mixed_ref[...] = total(0, WIDTH).astype(BF)
    rows_ref[...] = total(WIDTH, 2 * WIDTH).astype(BF)
    columns = total(2 * WIDTH, 2 * WIDTH + NOTES).T
    gates_ref[...] = columns[:TOP] + columns[TOP : 2 * TOP] + columns[2 * TOP : 3 * TOP]


def local(tokens, expert_ids, gate_values, w_gate, w_up, w_down, cotangent):
    total = 2 * WIDTH + NOTES
    place = lax.axis_index("expert")
    depth = (lax.axis_index("dp") * EXPERTS + place).astype(jnp.int32).reshape(1)
    spots = [PLANE_STEP * spot % PLANE for spot in range(PLANE)]
    levels = [DEPTH_STEP * level % DEPTH for level in range(DEPTH)]
    planes = [[spot * DEPTH + level for spot in spots] for level in range(DEPTH)]
    lines = [[spot * DEPTH + level for level in levels] for spot in range(PLANE)]

    planes += [[EXPERTS + member for member in group] for group in planes]
    lines += [[EXPERTS + member for member in group] for group in lines]

    def exchange(blocks, groups):
        return lax.all_to_all(
            blocks,
            ("dp", "expert"),
            split_axis=0,
            concat_axis=0,
            tiled=True,
            axis_index_groups=groups,
        )

    def near(array):
        return pltpu.with_memory_space_constraint(array, pltpu.VMEM)

    def far(array):
        return pltpu.with_memory_space_constraint(array, pltpu.HBM)

    vmem = pl.BlockSpec(memory_space=pltpu.VMEM)
    smem = pl.BlockSpec(memory_space=pltpu.SMEM)
    anywhere = pl.BlockSpec(memory_space=pl.ANY)
    packed = pl.pallas_call(
        pack_kernel,
        out_shape=pltpu.VMEM((LINE, total), BF),
        in_specs=[smem] + [anywhere] * 4,
        out_specs=vmem,
        scratch_shapes=[
            pltpu.VMEM((ROWS, WIDTH), BF),
            pltpu.VMEM((ROWS, WIDTH), BF),
            pltpu.VMEM((TOP, ROWS), jnp.int32),
            pltpu.VMEM((TOP, ROWS), F32),
            pltpu.SemaphoreType.DMA((4,)),
        ],
        name="pack",
        compiler_params=pltpu.CompilerParams(vmem_limit_bytes=8 * MIB),
    )(depth, far(tokens), far(cotangent), far(expert_ids.T), far(gate_values.T))
    line = near(exchange(packed.reshape(DEPTH, ROWS, total), lines).reshape(LINE, total))
    sent, weight, pick = pl.pallas_call(
        dispatch_kernel,
        out_shape=(
            pltpu.VMEM((SLOTS, 2 * WIDTH), BF),
            pltpu.VMEM((LINE, SLOTS), F32),
            pltpu.VMEM((LINE, SLOTS), F32),
        ),
        in_specs=[smem, vmem],
        out_specs=(vmem, vmem, vmem),
        name="dispatch",
        compiler_params=pltpu.CompilerParams(vmem_limit_bytes=16 * MIB),
    )(depth, line)
    received = exchange(sent.reshape(PLANE, EACH, 2 * WIDTH), planes)
    received = near(received.reshape(SLOTS, 2 * WIDTH))
    output = pl.pallas_call(
        expert_kernel,
        out_shape=pltpu.VMEM((SLOTS, 2 * WIDTH), BF),
        in_specs=[vmem, vmem, vmem, anywhere],
        out_specs=vmem,
        scratch_shapes=[
            pltpu.VMEM((HIDDEN, WIDTH), BF),
            pltpu.SemaphoreType.DMA,
        ],
        name="expert",
        compiler_params=pltpu.CompilerParams(vmem_limit_bytes=28 * MIB),
    )(received, near(w_gate[0]), near(w_up[0]), far(w_down[0]))
    back = exchange(output.reshape(PLANE, EACH, 2 * WIDTH), planes)
    back = near(back.reshape(SLOTS, 2 * WIDTH))
    parts = pl.pallas_call(
        combine_kernel,
        out_shape=pltpu.VMEM((LINE, total), BF),
        in_specs=[vmem] * 4,
        out_specs=vmem,
        name="combine",
        compiler_params=pltpu.CompilerParams(vmem_limit_bytes=16 * MIB),
    )(near(weight), near(pick), line, back)
    parts = near(exchange(parts.reshape(DEPTH, ROWS, total), lines))
    mixed_rows, row_grads, gate_grads = pl.pallas_call(
        finish_kernel,
        out_shape=(
            jax.ShapeDtypeStruct((ROWS, WIDTH), BF),
            jax.ShapeDtypeStruct((ROWS, WIDTH), BF),
            jax.ShapeDtypeStruct((TOP, ROWS), F32),
        ),
        in_specs=[vmem],
        out_specs=(vmem, vmem, vmem),
        name="finish",
        compiler_params=pltpu.CompilerParams(vmem_limit_bytes=8 * MIB),
    )(parts)
    return (mixed_rows, row_grads, gate_grads.T)


def solution(mesh):
    return jax.shard_map(
        local,
        mesh=mesh,
        in_specs=(
            P(("dp", "expert"), None),
            P(("dp", "expert"), None),
            P(("dp", "expert"), None),
            P("expert", None, None),
            P("expert", None, None),
            P("expert", None, None),
            P(("dp", "expert"), None),
        ),
        out_specs=(P(("dp", "expert"), None), P(("dp", "expert"), None), P(("dp", "expert"), None)),
        check_vma=False,
    )
```
